32 devices in a mesh: group: 1, ep: 8 (over z, y), tp: 4 (over x, core).
Axes of the slice: x: 2, y: 2, z: 4, core: 2. Of those that a mesh axis runs over, the one named last changes fastest.
Arguments:
- hidden_in: bfloat16 [32, 2, 4096], P('group', None, ('ep', 'tp')), may hold values from -6 to 6
- queries: bfloat16 [32, 2, 8192], P(('group', 'ep', 'tp')), may hold values from -128 to 128
- new_keys: bfloat16 [32, 2, 512], P(('group', 'ep', 'tp')), may hold values from -6 to 6
- new_values: bfloat16 [32, 2, 512], P(('group', 'ep', 'tp')), may hold values from -6 to 6
- key_cache: bfloat16 [24576, 512], P(('group', 'ep', 'tp')), may hold values from -6 to 6
- value_cache: bfloat16 [24576, 512], P(('group', 'ep', 'tp')), may hold values from -6 to 6
- cache_lengths: int32 [32], P(('group', 'ep', 'tp')), may hold values from 1 to 768, as said below
- page_table: int32 [32, 48], P(('group', 'ep', 'tp')), may hold values from 0 to 47, as said below
- o_proj: bfloat16 [8192, 4096], P(None, ('ep', 'tp')), may hold values from -0.0625 to 0.0625
- norm_gain: bfloat16 [4096], replicated, may hold values from 0.5 to 1.5
- expert_ids: int32 [2, 32, 8], P(None, 'group'), may hold values from 0 to 63, all different within a row; in each aligned block of 32 rows (0 to 31, 32 to 63, ..., all dimensions but the last counted through in order) at most 8 rows name the same one
- gate_scores: float32 [2, 32, 8], P(None, 'group'), may hold values from 0.1 to 1
- w_gate: bfloat16 [128, 4096, 384], P(('ep', 'tp')), may hold values from -0.09375 to 0.09375
- w_up: bfloat16 [128, 4096, 384], P(('ep', 'tp')), may hold values from -0.09375 to 0.09375
- w_down: bfloat16 [128, 384, 4096], P(('ep', 'tp')), may hold values from -0.21875 to 0.21875
Outputs:
- layer_out: bfloat16 [32, 2, 4096], P(('group', 'ep', 'tp'))
The draws below stay inside these ranges and needn't reach their ends.
Inputs may be any that keep to these rules, and one draw needn't show every extreme that they name: `cache_lengths`: request b's pages lie in the pool of device b (index over ep and tp together, ep slowest); the requests of one device hold at most 48 pages in all, and those of device i and of the device i + half the count of devices together hold 54 pages. `page_table`: row b lists every slot of its device's pool once; its first ceil(cache_lengths[b] / 16) entries are request b's pages in order; no two requests share a page. `expert_ids`: in each step no expert is named by more than 8 tokens.
All inputs are finite; a program needn't handle non-finite values.
Results may differ from the reference program's by a relative error of at most 0.008.
Values may be sent and summed in bfloat16 or wider, within the bound.
No kernel may reach another device: no remote copies, remote signals or barrier semaphores. Data moves between devices by JAX's collectives and lax.ppermute only.
A program may use at most 128 MiB of HBM per device.

```python
import math
import jax
import jax.numpy as jnp
import numpy as np
from jax import lax

D = 4096
HQ = 64
KVH = 4
HD = 128
EXPERTS = 64
FFE = 768
HALF = 384
TOP = 8
STEPS = 2
R_DEV = 1
POOL = 48
PAGE = 16
BATCH = 32
CAP = 8
N_EP = 8
N_TP = 4


def query_and_keys(key):
    pieces = jax.random.split(jax.random.fold_in(key, 31), 2)
    asked = jnp.clip(jax.random.normal(pieces[0], (BATCH, STEPS, HQ, HD), jnp.float32), -6.0, 6.0)
    probe = jnp.clip(jax.random.normal(pieces[1], (BATCH, STEPS, KVH, HD), jnp.float32), -6.0, 6.0)
    asked = jnp.clip(asked, -128.0, 128.0)
    probe = jnp.clip(probe, -6.0, 6.0)
    return (asked.reshape(BATCH, STEPS, HQ * HD).astype(jnp.bfloat16), probe.reshape(BATCH, STEPS, KVH * HD).astype(jnp.bfloat16))


def draw_queries(key, part):
    return query_and_keys(key)[0]


def draw_new_keys(key, part):
    return query_and_keys(key)[1]


def lengths_and_pages(key):
    device_count = N_EP * N_TP
    paired = device_count // 2
    pieces = jax.random.split(jax.random.fold_in(key, 57), 5)
    heavy = jax.random.randint(pieces[0], (paired,), 3 * POOL // 4, POOL + 1)
    light = 9 * POOL // 8 - heavy
    flipped = jax.random.randint(pieces[1], (paired,), 0, 2) == 1
    lower_side = jnp.where(flipped, heavy, light)
    upper_side = jnp.where(flipped, light, heavy)
    device_pages = jnp.concatenate([lower_side, upper_side])
    spread = jax.random.randint(pieces[2], (device_count, R_DEV), 1, 100)
    spare = device_pages - R_DEV
    shares = spare[:, None] * spread // jnp.sum(spread, 1, keepdims=True)
    leftover = spare - jnp.sum(shares, 1)
    shares = jnp.concatenate([shares[:, :-1], shares[:, -1:] + leftover[:, None]], axis=1)
    page_counts = 1 + shares
    trimmed = jax.random.randint(pieces[3], (device_count, R_DEV), 0, PAGE)
    lengths = page_counts * PAGE - trimmed
    shuffled = jax.vmap(lambda sub_key: jax.random.permutation(sub_key, POOL))(jax.random.split(pieces[4], device_count))
    starts = jnp.cumsum(page_counts, 1) - page_counts
    columns = (jnp.arange(POOL)[None, None, :] + starts[:, :, None]) % POOL
    table = jnp.take_along_axis(shuffled[:, None, :], columns, axis=2)
    return (lengths.reshape(BATCH).astype(jnp.int32), table.reshape(BATCH, POOL).astype(jnp.int32))


def draw_cache_lengths(key, part):
    return lengths_and_pages(key)[0]


def draw_page_table(key, part):
    return lengths_and_pages(key)[1]


def level_of(key, shape, cuts, low, top_value):
    gain, own = 1.0, jax.random.fold_in(key, 6)
    for axis_at, blocks in cuts:
        heights = jnp.exp(jax.random.uniform(jax.random.fold_in(own, axis_at), (blocks,), jnp.float32, low / len(cuts), top_value / len(cuts)))
        gain = gain * jnp.repeat(heights, shape[axis_at] // blocks).reshape([-1 if axis == axis_at else 1 for axis in range(len(shape))])
    return gain


def routed_block(stream_key, own, number, rows, count, top, bound, skew):
    order = jax.random.permutation(stream_key, count)
    packed, ordinary = portions_of(count, rows * top, bound, skew, True), portions_of(count, rows * top, bound, skew, False)
    places = jnp.arange(count)

    def named(tallies, rotation):
        used = int((tallies > 0).sum())
        fixed = max(1, used // 4)
        moved = fixed + (places - fixed + rotation * (used - fixed)) % max(1, count - fixed)
        return jnp.zeros((count,), jnp.int32).at[order[jnp.where(places < fixed, places, moved)]].set(jnp.asarray(tallies, jnp.int32))

    tallies = jnp.where(number % 4 == 0, named(packed, number // 4), named(ordinary, number - number // 4 - 1))
    mixed = jax.random.permutation(jax.random.fold_in(own, 3), count)
    giver, taker = mixed[0:count // 2 * 2:2], mixed[1:count // 2 * 2:2]
    room = jnp.minimum(tallies[giver] - 1, bound - tallies[taker]) // 2
    room = jnp.where((giver == order[0]) | (taker == order[0]) | (tallies[taker] == 0), 0, jnp.maximum(room, 0))
    moved = jax.random.randint(jax.random.fold_in(own, 4), (count // 2,), 0, 1 << 20) % (room + 1)
    tallies = tallies.at[giver].add(-moved).at[taker].add(moved)
    members = jnp.searchsorted(jnp.cumsum(tallies), jnp.arange(rows * top), side="right").astype(jnp.int32)
    table = members.reshape(top, rows).T
    table = table[jax.random.permutation(jax.random.fold_in(own, 1), rows)]
    rotation = jax.random.randint(jax.random.fold_in(own, 2), (rows, 1), 0, top)
    return jnp.take_along_axis(table, (jnp.arange(top)[None, :] + rotation) % top, axis=1)


def portions_of(number_of, total, bound, skew, full):
    weights = [(1 << 20) // math.isqrt(rank ** skew) + 1 for rank in range(1, number_of + 1)]
    largest = bound if full else min(bound, max(-(-total // number_of), total * weights[0] // sum(weights)))
    least = 1 if total - largest >= number_of - 1 else 0
    counts, rest = [largest] + [least] * (number_of - 1), total - largest - least * (number_of - 1)
    while rest > 0:
        free = [i for i in range(1, number_of) if counts[i] < largest] or [i for i in range(1, number_of) if counts[i] < bound]
        whole, left = sum([weights[i] for i in free]), rest
        for i in free:
            extra = min(bound - counts[i], max(1, left * weights[i] // whole), rest)
            counts[i] = counts[i] + extra
            rest = rest - extra
    return np.array(counts)


def scatter_about(key, shape, width, most, cuts=(), kind=jnp.bfloat16):
    values = width * jax.random.normal(key, shape, jnp.float32)
    if cuts:
        values = values * level_of(key, shape, cuts, -0.22, 0.18)
    return jnp.clip(values, -most, most).astype(kind)


def setup_inputs(seed: int = 0, part: int = 0) -> dict:
    key_of = jax.random.split(jax.random.key(seed), 16)
    own_keys = jax.random.split(jax.random.fold_in(key_of[15], part), 16)
    hidden_in = scatter_about(own_keys[0], (BATCH, STEPS, D), 1.0, 6.0, ((2, 32),))
    queries = draw_queries(jax.random.fold_in(jax.random.fold_in(key_of[15], part), 71), part)
    new_keys = draw_new_keys(jax.random.fold_in(jax.random.fold_in(key_of[15], part), 71), part)
    new_values = scatter_about(own_keys[3], (BATCH, STEPS, KVH * HD), 1.0, 6.0, ((0, 32),))
    key_cache = scatter_about(own_keys[4], (N_EP * N_TP * POOL * PAGE, KVH * HD), 1.0, 6.0, ((0, 32),))
    value_cache = scatter_about(own_keys[5], (N_EP * N_TP * POOL * PAGE, KVH * HD), 1.0, 6.0, ((0, 32),))
    cache_lengths = draw_cache_lengths(jax.random.fold_in(jax.random.fold_in(key_of[15], part), 71), part)
    page_table = draw_page_table(jax.random.fold_in(jax.random.fold_in(key_of[15], part), 71), part)
    o_proj = scatter_about(key_of[8], (HQ * HD, D), (HQ * HD) ** -0.5, 0.0625, ((1, 32),))
    norm_gain = jnp.clip(1.0 + 0.1 * jax.random.normal(key_of[9], (D,), jnp.float32), 0.5, 1.5).astype(jnp.bfloat16)
    expert_ids_keys = jax.random.split(jax.random.fold_in(own_keys[10], 1), STEPS * BATCH // BATCH)
    expert_ids_turns = jax.random.permutation(jax.random.fold_in(own_keys[10], 3), STEPS * BATCH // BATCH)
    expert_ids = jax.vmap(lambda own, number: routed_block(jax.random.fold_in(own_keys[10], 2), own, number, BATCH, EXPERTS, TOP, CAP, 2))(expert_ids_keys, expert_ids_turns).reshape((STEPS, BATCH, TOP))
    gate_scores = jnp.clip(jnp.exp(jax.random.uniform(own_keys[11], (STEPS, BATCH, TOP), jnp.float32, math.log(0.1), math.log(1.0))), 0.1, 1.0)
    w_gate = scatter_about(key_of[12], (2 * EXPERTS, D, HALF), D ** -0.5, 0.09375, ((0, 32),))
    w_up = scatter_about(key_of[13], (2 * EXPERTS, D, HALF), D ** -0.5, 0.09375, ((0, 32),))
    w_down = scatter_about(key_of[14], (2 * EXPERTS, HALF, D), FFE ** -0.5, 0.21875, ((0, 32),))
    return {"hidden_in": hidden_in, "queries": queries, "new_keys": new_keys, "new_values": new_values, "key_cache": key_cache, "value_cache": value_cache, "cache_lengths": cache_lengths, "page_table": page_table, "o_proj": o_proj, "norm_gain": norm_gain, "expert_ids": expert_ids, "gate_scores": gate_scores, "w_gate": w_gate, "w_up": w_up, "w_down": w_down}


def attend_request(query_rows, cached_keys, cached_values, fresh_keys, fresh_values, cache_size):
    step_count = query_rows.shape[0]
    groups = HQ // KVH
    scaling = 1.0 / HD ** 0.5
    asked = query_rows.astype(jnp.float32).reshape(step_count, KVH, groups, HD)
    old_keys = cached_keys.astype(jnp.float32).reshape(-1, KVH, HD)
    old_values = cached_values.astype(jnp.float32).reshape(-1, KVH, HD)
    new_keys_f = fresh_keys.astype(jnp.float32).reshape(step_count, KVH, HD)
    new_values_f = fresh_values.astype(jnp.float32).reshape(step_count, KVH, HD)
    cached_scores = jnp.einsum('sgqd,tgd->sgqt', asked, old_keys) * scaling
    fresh_scores = jnp.einsum('sgqd,tgd->sgqt', asked, new_keys_f) * scaling
    old_ok = (jnp.arange(old_keys.shape[0]) < cache_size)[None, None, None, :]
    positions = jnp.arange(step_count)
    new_ok = (positions[None, :] <= positions[:, None])[:, None, None, :]
    row_max = jnp.maximum(lax.optimization_barrier(jnp.max(jnp.where(old_ok, cached_scores, -1e+30), -1)), lax.optimization_barrier(jnp.max(jnp.where(new_ok, fresh_scores, -1e+30), -1)))
    old_weights = jnp.where(old_ok, jnp.exp(cached_scores - row_max[..., None]), 0.0)
    new_weights = jnp.where(new_ok, jnp.exp(fresh_scores - row_max[..., None]), 0.0)
    weight_sum = lax.optimization_barrier(jnp.sum(old_weights, -1)) + lax.optimization_barrier(jnp.sum(new_weights, -1))
    mixture = jnp.einsum('sgqt,tgd->sgqd', old_weights.astype(jnp.bfloat16).astype(jnp.float32), old_values)
    mixture = mixture + jnp.einsum('sgqt,tgd->sgqd', new_weights.astype(jnp.bfloat16).astype(jnp.float32), new_values_f)
    return (mixture / weight_sum[..., None]).astype(jnp.bfloat16).reshape(step_count, HQ * HD)

def reference(hidden_in, queries, new_keys, new_values, key_cache, value_cache, cache_lengths, page_table, o_proj, norm_gain, expert_ids, gate_scores, w_gate, w_up, w_down):
    batch_rows = queries.shape[0]
    step_count = queries.shape[1]
    key_pages = key_cache.reshape(-1, PAGE, KVH * HD)
    value_pages = value_cache.reshape(-1, PAGE, KVH * HD)

    def one_request(request):
        pool_rows = request // R_DEV * POOL + page_table[request]
        cached_keys = jnp.take(key_pages, pool_rows.astype(jnp.int32), axis=0).reshape(-1, KVH * HD)
        cached_values = jnp.take(value_pages, pool_rows.astype(jnp.int32), axis=0).reshape(-1, KVH * HD)
        return attend_request(queries[request], cached_keys, cached_values, new_keys[request], new_values[request], cache_lengths[request])
    attn_out = lax.map(one_request, jnp.arange(batch_rows, dtype=jnp.int32))
    projected = jnp.dot(attn_out.reshape(-1, HQ * HD), o_proj, preferred_element_type=jnp.float32)
    residual = (hidden_in.astype(jnp.float32) + projected.reshape(batch_rows, step_count, D)).astype(jnp.bfloat16)
    widened = residual.astype(jnp.float32)
    inverse = lax.rsqrt(lax.optimization_barrier(jnp.mean(widened * widened, -1, keepdims=True)) + 1e-06)
    normed = (widened * inverse * norm_gain.astype(jnp.float32)).astype(jnp.bfloat16)
    flattened = normed.reshape(-1, D)
    gates = gate_scores / lax.optimization_barrier(jnp.sum(gate_scores, -1, keepdims=True))
    gate_halves = w_gate.reshape(EXPERTS, 2, D, HALF)
    up_halves = w_up.reshape(EXPERTS, 2, D, HALF)
    down_halves = w_down.reshape(EXPERTS, 2, HALF, D)

    def one_expert(carried, expert):
        gate_full = jnp.concatenate([gate_halves[expert, 0], gate_halves[expert, 1]], axis=1)
        up_full = jnp.concatenate([up_halves[expert, 0], up_halves[expert, 1]], axis=1)
        down_full = jnp.concatenate([down_halves[expert, 0], down_halves[expert, 1]], axis=0)
        gate_act = jnp.dot(flattened, gate_full, preferred_element_type=jnp.float32)
        up_act = jnp.dot(flattened, up_full, preferred_element_type=jnp.float32)
        hidden = (jax.nn.silu(gate_act) * up_act).astype(jnp.bfloat16)
        expert_out = jnp.dot(hidden, down_full, preferred_element_type=jnp.float32).reshape(batch_rows, step_count, D)
        gate_share = lax.optimization_barrier(jnp.sum(jnp.where(expert_ids == expert, gates, 0.0), -1)).T
        return (carried + gate_share[..., None] * expert_out, None)
    start_sum = jnp.zeros((batch_rows, step_count, D), jnp.float32)
    expert_sum, unused = lax.scan(one_expert, start_sum, jnp.arange(EXPERTS, dtype=jnp.int32))
    return (widened + expert_sum).astype(jnp.bfloat16)
```

```python
import functools
import math

import jax
import jax.numpy as jnp
from jax import lax
from jax.experimental import pallas as pl
from jax.experimental.pallas import tpu as pltpu
from jax.sharding import PartitionSpec as P

HQ = 64
KVH = 4
HD = 128
PAGE = 16
CORES = 2
AXES = ("ep", "tp")
MIB = 1 << 20

masked_score = -1e30


VM = pl.BlockSpec(memory_space=pltpu.VMEM)
SM = pl.BlockSpec(memory_space=pltpu.SMEM)
ANY = pl.BlockSpec(memory_space=pl.ANY)


class Geometry:
    def __init__(self, ep, tp):
        self.far = 4 if ep % 4 == 0 else (2 if ep % 2 == 0 else 1)
        self.near = ep // self.far
        self.side = tp // CORES
        self.columns = self.near * self.side
        self.places = self.far * self.columns
        self.shifts = [(a, b) for a in range(self.near) for b in range(self.side)]

    def index(self, far, near, side, core):
        return ((far * self.near + near) * self.side + side) * CORES + core

    def everyone(self):
        for far in range(self.far):
            for near in range(self.near):
                for side in range(self.side):
                    for core in range(CORES):
                        yield far, near, side, core

    def along_far(self, step):
        return [
            (self.index(f, n, s, c), self.index((f + step) % self.far, n, s, c))
            for f, n, s, c in self.everyone()
        ]

    def along_column(self, shift):
        return [
            (
                self.index(f, n, s, c),
                self.index(f, (n + shift[0]) % self.near, (s + shift[1]) % self.side, c),
            )
            for f, n, s, c in self.everyone()
        ]

    def to_partner(self):
        return [(self.index(f, n, s, c), self.index(f, n, s, 1 - c)) for f, n, s, c in self.everyone()]

    def here(self):
        ep, tp = lax.axis_index("ep"), lax.axis_index("tp")
        far, near = lax.div(ep, self.near), lax.rem(ep, self.near)
        side, core = lax.div(tp, CORES), lax.rem(tp, CORES)
        return far, near, side, core

    def column_at(self, near, side, shift, sign):
        a = lax.rem(near + sign * shift[0] + self.near, self.near)
        b = lax.rem(side + sign * shift[1] + self.side, self.side)
        return a * self.side + b

    def in_order(self, stacked):
        far, near, side, core = self.here()
        place = jnp.arange(self.places, dtype=jnp.int32)
        step = (far - place // self.columns) % self.far
        a = (near - place // self.side % self.near) % self.near
        b = (side - place % self.side) % self.side
        slot = (a * self.side + b) * self.far + step
        rows, span = stacked.shape[-2:]
        ordered = jnp.take(stacked.reshape(self.places, rows, span), slot, axis=0)
        return ordered.transpose(1, 0, 2).reshape(rows, self.places * span)

    def far_at(self, far, step, sign):
        return lax.rem(far + sign * step + self.far, self.far)


def in_vmem(array):
    return pltpu.with_memory_space_constraint(array, pltpu.VMEM)


def call(kernel, name, out_shape, in_specs, scratch=(), limit=8, flops=0, nbytes=0):
    single = not isinstance(out_shape, (list, tuple))
    return pl.pallas_call(
        kernel,
        name=name,
        out_shape=out_shape,
        in_specs=in_specs,
        out_specs=VM if single else [VM] * len(out_shape),
        scratch_shapes=scratch,
        compiler_params=pltpu.CompilerParams(vmem_limit_bytes=limit * MIB),
        cost_estimate=pl.CostEstimate(flops=flops, bytes_accessed=nbytes, transcendentals=0),
    )


def attention_kernel(
    steps, lens_ref, table_ref, q_ref, nk_ref, nv_ref, k_hbm, v_hbm, o_ref, kbuf, vbuf, sems
):
    pool = k_hbm.shape[0]
    requests, pages = table_ref.shape
    tokens = nk_ref.shape[0]
    width = k_hbm.shape[1]
    pad = kbuf.shape[0] - pool
    copy_k = pltpu.make_async_copy(k_hbm, kbuf.at[pl.ds(0, pool)], sems.at[0])
    copy_v = pltpu.make_async_copy(v_hbm, vbuf.at[pl.ds(0, pool)], sems.at[1])
    copy_k.start()
    copy_v.start()
    kbuf[pool:, :] = jnp.zeros((pad, width), kbuf.dtype)
    vbuf[pool:, :] = jnp.zeros((pad, width), vbuf.dtype)
    kbuf[pool : pool + tokens, :] = nk_ref[...]
    vbuf[pool : pool + tokens, :] = nv_ref[...]
    group_rows = q_ref.shape[0] // KVH
    row = lax.rem(lax.broadcasted_iota(jnp.int32, (group_rows, 1), 0), tokens)
    row_request = lax.div(row, steps)
    row_step = lax.rem(row, steps)
    eye = lax.broadcasted_iota(jnp.int32, (pages, pages), 0) == lax.broadcasted_iota(
        jnp.int32, (pages, pages), 1
    )
    token = lax.broadcasted_iota(jnp.int32, (pages, pool), 1)
    slot = lax.div(token, PAGE)
    offset = lax.rem(token, PAGE)
    slot_f = slot.astype(jnp.float32)
    page = lax.broadcasted_iota(jnp.int32, (pages, 1), 0)
    cached = jnp.zeros((group_rows, pool), jnp.float32)
    for r in range(requests):
        slots = table_ref[r : r + 1, :].astype(jnp.float32)
        slots = jnp.sum(jnp.where(eye, slots, 0.0), axis=1, keepdims=True)
        hit = (slot_f == slots) & (offset < lens_ref[r] - page * PAGE)
        valid = jnp.max(jnp.where(hit, 1.0, 0.0), axis=0, keepdims=True)
        cached = jnp.where(row_request == r, valid, cached)
    fresh = lax.broadcasted_iota(jnp.int32, (group_rows, pad), 1)
    fresh_ok = (
        (fresh < tokens)
        & (lax.div(fresh, steps) == row_request)
        & (lax.rem(fresh, steps) <= row_step)
    )
    allowed = jnp.concatenate([cached, jnp.where(fresh_ok, 1.0, 0.0)], axis=1) > 0.5
    scaling = 1.0 / HD**0.5
    copy_k.wait()
    weights, sums = [], []
    for g in range(KVH):
        scores = (
            lax.dot_general(
                q_ref[g * group_rows : (g + 1) * group_rows, :],
                kbuf[:, g * HD : (g + 1) * HD],
                (((1,), (1,)), ((), ())),
                preferred_element_type=jnp.float32,
            )
            * scaling
        )
        scores = jnp.where(allowed, scores, masked_score)
        highest = jnp.max(scores, axis=1, keepdims=True)
        weight = jnp.exp(scores - highest)
        sums.append(jnp.sum(weight, axis=1, keepdims=True))
        weights.append(weight.astype(jnp.bfloat16))
    copy_v.wait()
    for g in range(KVH):
        mixture = jnp.dot(
            weights[g], vbuf[:, g * HD : (g + 1) * HD], preferred_element_type=jnp.float32
        )
        o_ref[g * group_rows : (g + 1) * group_rows, :] = (mixture / sums[g]).astype(o_ref.dtype)


def stack_kernel(count, *refs):
    o_ref = refs[-1]
    for i in range(count):
        o_ref[i] = refs[i][...]


def bring_kernel(after_ref, w_hbm, o_ref, sems):
    parts = sems.shape[0]
    rows = w_hbm.shape[0] // parts
    copies = []
    for i in range(parts):
        span = pl.ds(i * rows, rows)
        copies.append(pltpu.make_async_copy(w_hbm.at[span], o_ref.at[span], sems.at[i]))
    for copy in copies:
        copy.start()
    for copy in copies:
        copy.wait()


def project_kernel(geo, tokens, *refs):
    pieces = refs[: geo.columns]
    w_own, w_partner, h_own, h_partner, o_ref, wide, lhs = refs[geo.columns :]
    far, near, side, core = geo.here()
    rows = pieces[0].shape[1]
    width = w_own.shape[1]
    for q, shift in enumerate(geo.shifts):
        column = geo.column_at(near, side, shift, -1)
        for step in range(geo.far):
            place = geo.far_at(far, step, -1) * geo.columns + column
            start = pl.multiple_of(place * rows, rows)
            wide[pl.ds(start, rows), :] = pieces[q][step].astype(jnp.float32)
    for h in range(rows // tokens):
        for t in range(tokens):
            picked = wide[pl.ds(h * tokens + t, geo.places, stride=rows), :]
            lhs[t * geo.places : (t + 1) * geo.places, h * HD : (h + 1) * HD] = picked.astype(
                jnp.bfloat16
            )
    sums = []
    for weight, hidden in ((w_own, h_own), (w_partner, h_partner)):
        projected = jnp.dot(lhs[...], weight[...], preferred_element_type=jnp.float32)
        sums.append(hidden[...].astype(jnp.float32) + projected)
    if width % 128 == 0:
        for total, where in zip(sums, (core, 1 - core)):
            start = pl.multiple_of(where * width, width)
            o_ref[:, pl.ds(start, width)] = total.astype(o_ref.dtype)
    else:
        straight = jnp.concatenate(sums, axis=1)
        crossed = jnp.concatenate(sums[::-1], axis=1)
        o_ref[...] = jnp.where(core == 0, straight, crossed).astype(o_ref.dtype)


def norm_kernel(geo, tokens, *refs):
    pieces = refs[:-4]
    gain, n_ref, r_ref, wide = refs[-4:]
    far, near, side, core = geo.here()
    depth = wide.shape[1]
    span = pieces[0].shape[2]
    if len(pieces) == 1:
        wide[...] = pieces[0][0].astype(jnp.float32)
    for q, shift in enumerate(geo.shifts if len(pieces) > 1 else ()):
        column = geo.column_at(near, side, shift, -1)
        for step in range(geo.far):
            place = geo.far_at(far, step, -1) * geo.columns + column
            start = pl.multiple_of(place * span, span)
            wide[:, pl.ds(start, span)] = pieces[q][step].astype(jnp.float32)
    values = wide[...]
    inverse = lax.rsqrt(jnp.sum(values * values, axis=1, keepdims=True) / depth + 1e-06)
    n_ref[...] = (values * inverse * gain[...].astype(jnp.float32)).astype(n_ref.dtype)
    me = far * geo.columns + near * geo.side + side
    for t in range(tokens):
        r_ref[t : t + 1, :] = wide[pl.ds(t * geo.places + me, 1), :]


def expert_kernel(geo, x_own, x_partner, ids, scores, wg, wu, wd, keep, send, lhs, hid):
    half = x_own.shape[0]
    lhs[:half, :] = x_own[...]
    lhs[half:, :] = x_partner[...]
    far, near, side, core = geo.here()
    local = wg.shape[0]
    width = wg.shape[2]
    first = geo.index(far, near, side, core) * local
    gates = scores[...] / jnp.sum(scores[...], axis=1, keepdims=True)
    chosen = ids[...]
    for j in range(local):
        share = jnp.sum(
            jnp.where(chosen == lax.div(first + j, 2), gates, 0.0), axis=1, keepdims=True
        )
        gate = jnp.dot(lhs[...], wg[j], preferred_element_type=jnp.float32)
        up = jnp.dot(lhs[...], wu[j], preferred_element_type=jnp.float32)
        hidden = gate / (1.0 + jnp.exp(-gate)) * up * share
        hid[:, j * width : (j + 1) * width] = hidden.astype(jnp.bfloat16)
    chunk = 512
    for n in range(wd.shape[1] // chunk):
        span = slice(n * chunk, (n + 1) * chunk)
        out = jnp.dot(hid[...], wd[:, span], preferred_element_type=jnp.float32)
        keep[:, span] = out[:half]
        send[:, span] = out[half:].astype(send.dtype)


def column_sum_kernel(geo, tokens, *refs):
    kept, received = refs[:2]
    outs, wide = refs[2:-1], refs[-1]
    far, near, side, core = geo.here()
    starts = [geo.column_at(near, side, shift, 1) for shift in geo.shifts]
    for k in range(wide.shape[0]):
        lanes = slice(k * 128, (k + 1) * 128)
        wide[k] = kept[:, lanes] + received[:, lanes].astype(jnp.float32)
        for q, start in enumerate(starts):
            picked = wide[k, pl.ds(start, tokens * geo.far, stride=geo.columns), :]
            outs[q][:, lanes] = picked.astype(outs[q].dtype)


def far_sum_kernel(geo, tokens, *refs):
    ins = refs[: geo.columns]
    outs, wide = refs[geo.columns : -1], refs[-1]
    far, near, side, core = geo.here()
    starts = [geo.far_at(far, step, 1) for step in range(geo.far)]
    for k in range(wide.shape[0]):
        lanes = slice(k * 128, (k + 1) * 128)
        total = ins[0][:, lanes]
        for other in ins[1:]:
            total = total + other[:, lanes].astype(jnp.float32)
        wide[k] = total
        for step, start in enumerate(starts):
            picked = wide[k, pl.ds(start, tokens, stride=geo.far), :]
            outs[step][:, lanes] = picked.astype(outs[step].dtype)


def final_kernel(*refs):
    o_ref = refs[-1]
    total = refs[0][...]
    for other in refs[1:-1]:
        total = total + other[...].astype(jnp.float32)
    o_ref[...] = total.astype(o_ref.dtype)


def body(
    geo,
    hidden_in,
    queries,
    new_keys,
    new_values,
    key_cache,
    value_cache,
    cache_lengths,
    page_table,
    o_proj,
    norm_gain,
    expert_ids,
    gate_scores,
    w_gate,
    w_up,
    w_down,
):
    requests, steps = queries.shape[:2]
    tokens = requests * steps
    depth = norm_gain.shape[0]
    col_width = hidden_in.shape[2]
    places = geo.places
    top = expert_ids.shape[2]
    bf16, f32 = jnp.bfloat16, jnp.float32
    far, near, side, core = geo.here()

    def swap(array):
        return lax.ppermute(array, AXES, geo.to_partner())

    o_partner = swap(o_proj)
    hidden = hidden_in.reshape(places, CORES, requests, steps, col_width)
    hidden = hidden.transpose(1, 2, 3, 0, 4).reshape(CORES, tokens * places, col_width)
    h_own = jnp.where(core == 0, hidden[0], hidden[1])
    h_partner = swap(jnp.where(core == 0, hidden[1], hidden[0]))

    def rows_of(array):
        array = array.reshape(steps, places, CORES, requests, top).transpose(2, 3, 0, 1, 4)
        array = array.reshape(CORES, tokens * places, top)
        array = jnp.where(core == 0, array, array[::-1])
        return array.reshape(CORES * tokens * places, top)

    ids, scores = rows_of(expert_ids), rows_of(gate_scores)

    rows = HQ * tokens
    q = queries.reshape(tokens, HQ, HD).transpose(1, 0, 2).reshape(rows, HD)
    pool = key_cache.shape[0]
    padded = pool + 128 * -(-tokens // 128)
    attended = call(
        functools.partial(attention_kernel, steps),
        "attention",
        jax.ShapeDtypeStruct((rows, HD), bf16),
        [SM, VM, VM, VM, VM, ANY, ANY],
        [
            pltpu.VMEM((padded, key_cache.shape[1]), bf16),
            pltpu.VMEM((padded, key_cache.shape[1]), bf16),
            pltpu.SemaphoreType.DMA((2,)),
        ],
        nbytes=2 * key_cache.size * 2,
    )(
        cache_lengths,
        page_table,
        q,
        new_keys.reshape(tokens, -1),
        new_values.reshape(tokens, -1),
        key_cache,
        value_cache,
    )

    def gather_far(piece, after, weight):
        got = [piece] + [lax.ppermute(piece, AXES, geo.along_far(s)) for s in range(1, geo.far)]
        return call(
            functools.partial(stack_kernel, geo.far),
            "stack",
            jax.ShapeDtypeStruct((geo.far,) + piece.shape, piece.dtype),
            [VM] * geo.far,
        )(*got)

    def gather_column(stacked):
        return [stacked] + [
            lax.ppermute(stacked, AXES, geo.along_column(shift)) for shift in geo.shifts[1:]
        ]

    stacked = gather_far(attended, None, None)
    pieces = gather_column(stacked)
    residual = call(
        functools.partial(project_kernel, geo, tokens),
        "project",
        jax.ShapeDtypeStruct((tokens * places, CORES * col_width), bf16),
        [VM] * (geo.columns + 4),
        [
            pltpu.VMEM((places * rows, HD), f32),
            pltpu.VMEM((tokens * places, HQ * HD), bf16),
        ],
        limit=16,
    )(*pieces, o_proj, o_partner, h_own, h_partner)
    pieces = gather_column(gather_far(residual, None, None))
    if CORES * col_width % 128:
        pieces = [geo.in_order(jnp.stack(pieces))[None]]
    normed, own_residual = call(
        functools.partial(norm_kernel, geo, tokens),
        "norm",
        [
            jax.ShapeDtypeStruct((tokens * places, depth), bf16),
            jax.ShapeDtypeStruct((tokens, depth), f32),
        ],
        [VM] * (len(pieces) + 1),
        [pltpu.VMEM((tokens * places, depth), f32)],
        limit=16,
    )(*pieces, norm_gain.reshape(1, depth))
    normed_partner = swap(normed)
    local, half = w_gate.shape[0], w_gate.shape[2]
    keep, send = call(
        functools.partial(expert_kernel, geo),
        "experts",
        [
            jax.ShapeDtypeStruct((tokens * places, depth), f32),
            jax.ShapeDtypeStruct((tokens * places, depth), bf16),
        ],
        [VM] * 7,
        [
            pltpu.VMEM((CORES * tokens * places, depth), bf16),
            pltpu.VMEM((CORES * tokens * places, local * half), bf16),
        ],
        limit=16,
    )(
        normed,
        normed_partner,
        ids,
        scores,
        in_vmem(w_gate),
        in_vmem(w_up),
        in_vmem(w_down.reshape(local * half, depth)),
    )
    received = swap(send)
    parts = call(
        functools.partial(column_sum_kernel, geo, tokens),
        "column_sum",
        [
            jax.ShapeDtypeStruct((tokens * geo.far, depth), f32 if q == 0 else bf16)
            for q in range(geo.columns)
        ],
        [VM, VM],
        [pltpu.VMEM((depth // 128, tokens * places, 128), f32)],
    )(keep, received)
    parts = [parts[0]] + [
        lax.ppermute(part, AXES, geo.along_column(shift))
        for part, shift in zip(parts[1:], geo.shifts[1:])
    ]
    parts = call(
        functools.partial(far_sum_kernel, geo, tokens),
        "far_sum",
        [
            jax.ShapeDtypeStruct((tokens, depth), f32 if s == 0 else bf16)
            for s in range(geo.far)
        ],
        [VM] * geo.columns,
        [pltpu.VMEM((depth // 128, tokens * geo.far, 128), f32)],
    )(*parts)
    parts = [parts[0]] + [
        lax.ppermute(part, AXES, geo.along_far(step + 1)) for step, part in enumerate(parts[1:])
    ]
    out = call(
        final_kernel,
        "final",
        jax.ShapeDtypeStruct((tokens, depth), bf16),
        [VM] * (geo.far + 1),
    )(own_residual, *parts)
    return out.reshape(requests, steps, depth)


def solution(mesh):
    geo = Geometry(mesh.shape["ep"], mesh.shape["tp"])
    in_specs = (
        P("group", None, ("ep", "tp")),
        P(("group", "ep", "tp"), None, None),
        P(("group", "ep", "tp"), None, None),
        P(("group", "ep", "tp"), None, None),
        P(("group", "ep", "tp"), None),
        P(("group", "ep", "tp"), None),
        P(("group", "ep", "tp")),
        P(("group", "ep", "tp"), None),
        P(None, ("ep", "tp")),
        P(),
        P(None, "group", None),
        P(None, "group", None),
        P(("ep", "tp"), None, None),
        P(("ep", "tp"), None, None),
        P(("ep", "tp"), None, None),
    )
    out_specs = P(("group", "ep", "tp"), None, None)
    return jax.shard_map(
        functools.partial(body, geo),
        mesh=mesh,
        in_specs=in_specs,
        out_specs=out_specs,
        check_vma=False,
    )
```

```python
import functools
import math

import jax
import jax.numpy as jnp
from jax import lax
from jax.experimental import pallas as pl
from jax.experimental.pallas import tpu as pltpu
from jax.sharding import PartitionSpec as P

HQ = 64
KVH = 4
HD = 128
PAGE = 16
CORES = 2
AXES = ("ep", "tp")
MIB = 1 << 20
COST_FLOPS = 3 * 10**9

masked_score = -1e30


VM = pl.BlockSpec(memory_space=pltpu.VMEM)
SM = pl.BlockSpec(memory_space=pltpu.SMEM)
HBM = pl.BlockSpec(memory_space=pltpu.HBM)


class Geometry:
    def __init__(self, ep, tp):
        self.far = 4 if ep % 4 == 0 else (2 if ep % 2 == 0 else 1)
        self.near = ep // self.far
        self.side = tp // CORES
        self.columns = self.near * self.side
        self.places = self.far * self.columns
        self.shifts = [(a, b) for a in range(self.near) for b in range(self.side)]

    def index(self, far, near, side, core):
        return ((far * self.near + near) * self.side + side) * CORES + core

    def everyone(self):
        for far in range(self.far):
            for near in range(self.near):
                for side in range(self.side):
                    for core in range(CORES):
                        yield far, near, side, core

    def along_far(self, step):
        return [
            (self.index(f, n, s, c), self.index((f + step) % self.far, n, s, c))
            for f, n, s, c in self.everyone()
        ]

    def along_column(self, shift):
        return [
            (
                self.index(f, n, s, c),
                self.index(f, (n + shift[0]) % self.near, (s + shift[1]) % self.side, c),
            )
            for f, n, s, c in self.everyone()
        ]

    def to_partner(self):
        return [(self.index(f, n, s, c), self.index(f, n, s, 1 - c)) for f, n, s, c in self.everyone()]

    def here(self):
        ep, tp = lax.axis_index("ep"), lax.axis_index("tp")
        far, near = lax.div(ep, self.near), lax.rem(ep, self.near)
        side, core = lax.div(tp, CORES), lax.rem(tp, CORES)
        return far, near, side, core

    def column_at(self, near, side, shift, sign):
        a = lax.rem(near + sign * shift[0] + self.near, self.near)
        b = lax.rem(side + sign * shift[1] + self.side, self.side)
        return a * self.side + b

    def in_order(self, stacked):
        far, near, side, core = self.here()
        place = jnp.arange(self.places, dtype=jnp.int32)
        step = (far - place // self.columns) % self.far
        a = (near - place // self.side % self.near) % self.near
        b = (side - place % self.side) % self.side
        slot = (a * self.side + b) * self.far + step
        rows, span = stacked.shape[-2:]
        ordered = jnp.take(stacked.reshape(self.places, rows, span), slot, axis=0)
        return ordered.transpose(1, 0, 2).reshape(rows, self.places * span)

    def far_at(self, far, step, sign):
        return lax.rem(far + sign * step + self.far, self.far)


def in_vmem(array):
    return pltpu.with_memory_space_constraint(array, pltpu.VMEM)


def in_hbm(array):
    return pltpu.with_memory_space_constraint(array, pltpu.HBM)


def call(kernel, name, out_shape, in_specs, scratch=()):
    held = sum(
        math.prod(ref.shape) * jnp.dtype(ref.dtype).itemsize
        for ref in scratch
        if ref.memory_space == pltpu.VMEM
    )
    single = not isinstance(out_shape, (list, tuple))
    return pl.pallas_call(
        kernel,
        name=name,
        out_shape=out_shape,
        in_specs=in_specs,
        out_specs=VM if single else [VM] * len(out_shape),
        scratch_shapes=scratch,
        compiler_params=pltpu.CompilerParams(vmem_limit_bytes=held + 3 * MIB),
        cost_estimate=pl.CostEstimate(flops=COST_FLOPS, bytes_accessed=0, transcendentals=0),
    )


def attention_kernel(steps, *refs):
    lens_ref, sources, o_ref, buffers = refs[0], refs[1:7], refs[7], refs[8:]
    table_ref, q_ref, nk_ref, nv_ref, kbuf, vbuf, sems = buffers
    pool, width = sources[4].shape
    requests, pages = table_ref.shape
    tokens = nk_ref.shape[0]
    pad = kbuf.shape[0] - pool
    places = [table_ref, q_ref, nk_ref, nv_ref]
    places += [kbuf.at[pl.ds(0, pool)], vbuf.at[pl.ds(0, pool)]]
    copies = [
        pltpu.make_async_copy(source, place, sems.at[i])
        for i, (source, place) in enumerate(zip(sources, places))
    ]
    for copy in copies:
        copy.start()
    kbuf[pool:, :] = jnp.zeros((pad, width), kbuf.dtype)
    vbuf[pool:, :] = jnp.zeros((pad, width), vbuf.dtype)
    for copy in copies[:4]:
        copy.wait()
    kbuf[pool : pool + tokens, :] = nk_ref[...]
    vbuf[pool : pool + tokens, :] = nv_ref[...]
    group_rows = q_ref.shape[0] // KVH
    row = lax.rem(lax.broadcasted_iota(jnp.int32, (group_rows, 1), 0), tokens)
    row_request = lax.div(row, steps)
    row_step = lax.rem(row, steps)
    eye = lax.broadcasted_iota(jnp.int32, (pages, pages), 0) == lax.broadcasted_iota(
        jnp.int32, (pages, pages), 1
    )
    token = lax.broadcasted_iota(jnp.int32, (pages, pool), 1)
    slot = lax.div(token, PAGE)
    offset = lax.rem(token, PAGE)
    slot_f = slot.astype(jnp.float32)
    page = lax.broadcasted_iota(jnp.int32, (pages, 1), 0)
    cached = jnp.zeros((group_rows, pool), jnp.float32)
    for r in range(requests):
        slots = table_ref[r : r + 1, :].astype(jnp.float32)
        slots = jnp.sum(jnp.where(eye, slots, 0.0), axis=1, keepdims=True)
        hit = (slot_f == slots) & (offset < lens_ref[r] - page * PAGE)
        valid = jnp.max(jnp.where(hit, 1.0, 0.0), axis=0, keepdims=True)
        cached = jnp.where(row_request == r, valid, cached)
    fresh = lax.broadcasted_iota(jnp.int32, (group_rows, pad), 1)
    fresh_ok = (
        (fresh < tokens)
        & (lax.div(fresh, steps) == row_request)
        & (lax.rem(fresh, steps) <= row_step)
    )
    allowed = jnp.concatenate([cached, jnp.where(fresh_ok, 1.0, 0.0)], axis=1) > 0.5
    scaling = 1.0 / HD**0.5
    copies[4].wait()
    weights, sums = [], []
    for g in range(KVH):
        scores = (
            lax.dot_general(
                q_ref[g * group_rows : (g + 1) * group_rows, :],
                kbuf[:, g * HD : (g + 1) * HD],
                (((1,), (1,)), ((), ())),
                preferred_element_type=jnp.float32,
            )
            * scaling
        )
        scores = jnp.where(allowed, scores, masked_score)
        highest = jnp.max(scores, axis=1, keepdims=True)
        weight = jnp.exp(scores - highest)
        sums.append(jnp.sum(weight, axis=1, keepdims=True))
        weights.append(weight.astype(jnp.bfloat16))
    copies[5].wait()
    for g in range(KVH):
        mixture = jnp.dot(
            weights[g], vbuf[:, g * HD : (g + 1) * HD], preferred_element_type=jnp.float32
        )
        o_ref[g * group_rows : (g + 1) * group_rows, :] = (mixture / sums[g]).astype(o_ref.dtype)


def stack_kernel(count, *refs):
    o_ref = refs[-1]
    for i in range(count):
        o_ref[i] = refs[i][...]


def project_kernel(geo, tokens, *refs):
    pieces = refs[: geo.columns]
    w_own, w_partner, h_own, h_partner, o_ref, wide, lhs, hidden = refs[geo.columns :]
    far, near, side, core = geo.here()
    rows = pieces[0].shape[1]
    width = w_own.shape[1]
    for q, shift in enumerate(geo.shifts):
        column = geo.column_at(near, side, shift, -1)
        for step in range(geo.far):
            place = geo.far_at(far, step, -1) * geo.columns + column
            start = pl.multiple_of(place * rows, rows)
            wide[pl.ds(start, rows), :] = pieces[q][step].astype(jnp.float32)
    for h in range(rows // tokens):
        for t in range(tokens):
            picked = wide[pl.ds(h * tokens + t, geo.places, stride=rows), :]
            lhs[t * geo.places : (t + 1) * geo.places, h * HD : (h + 1) * HD] = picked.astype(
                jnp.bfloat16
            )
    sums = []
    for weight, arriving in ((w_own, h_own), (w_partner, h_partner)):
        projected = jnp.dot(lhs[...], weight[...], preferred_element_type=jnp.float32)
        if arriving.shape[0] == projected.shape[0]:
            mine = arriving[...].astype(jnp.float32)
        else:
            hidden[...] = arriving[...].astype(jnp.float32)
            mine = [
                hidden[pl.ds(core * tokens + t, geo.places, stride=CORES * tokens), :]
                for t in range(tokens)
            ]
            mine = jnp.concatenate(mine, axis=0)
        sums.append(mine + projected)
    if width % 128 == 0:
        for total, where in zip(sums, (core, 1 - core)):
            start = pl.multiple_of(where * width, width)
            o_ref[:, pl.ds(start, width)] = total.astype(o_ref.dtype)
    else:
        straight = jnp.concatenate(sums, axis=1)
        crossed = jnp.concatenate(sums[::-1], axis=1)
        o_ref[...] = jnp.where(core == 0, straight, crossed).astype(o_ref.dtype)


def norm_kernel(geo, tokens, *refs):
    pieces = refs[:-4]
    gain, n_ref, r_ref, wide = refs[-4:]
    far, near, side, core = geo.here()
    depth = wide.shape[1]
    span = pieces[0].shape[2]
    if len(pieces) == 1:
        wide[...] = pieces[0][0].astype(jnp.float32)
    for q, shift in enumerate(geo.shifts if len(pieces) > 1 else ()):
        column = geo.column_at(near, side, shift, -1)
        for step in range(geo.far):
            place = geo.far_at(far, step, -1) * geo.columns + column
            start = pl.multiple_of(place * span, span)
            wide[:, pl.ds(start, span)] = pieces[q][step].astype(jnp.float32)
    values = wide[...]
    inverse = lax.rsqrt(jnp.sum(values * values, axis=1, keepdims=True) / depth + 1e-06)
    for k in range(depth // 128):
        lanes = slice(k * 128, (k + 1) * 128)
        scale = gain[k : k + 1, :].astype(jnp.float32)
        n_ref[:, lanes] = (wide[:, lanes] * inverse * scale).astype(n_ref.dtype)
    me = far * geo.columns + near * geo.side + side
    for t in range(tokens):
        r_ref[t : t + 1, :] = wide[pl.ds(t * geo.places + me, 1), :]


def expert_kernel(geo, x_own, x_partner, ids, scores, wg, wu, wd, keep, send, lhs, hid):
    half = x_own.shape[0]
    lhs[:half, :] = x_own[...]
    lhs[half:, :] = x_partner[...]
    far, near, side, core = geo.here()
    local = wg.shape[0]
    width = wg.shape[2]
    first = geo.index(far, near, side, core) * local
    steps, batch = ids.shape[0], ids.shape[2]
    tokens = half // geo.places
    requests = tokens // steps
    row = lax.broadcasted_iota(jnp.int32, (CORES * half, batch), 0)
    lane = lax.broadcasted_iota(jnp.int32, (CORES * half, batch), 1)
    owner = jnp.where(row < half, core, 1 - core)
    inner = lax.rem(row, half)
    turn, place = lax.div(inner, geo.places), lax.rem(inner, geo.places)
    request, step = lax.div(turn, steps), lax.rem(turn, steps)
    belongs = lane == (place * CORES + owner) * requests + request
    chosen = [ids[s] for s in range(steps)]
    gates = [scores[s] / jnp.sum(scores[s], axis=0, keepdims=True) for s in range(steps)]

    def share_of(expert):
        total = jnp.zeros((CORES * half, batch), jnp.float32)
        for s in range(steps):
            named = jnp.where(chosen[s] == expert, gates[s], 0.0)
            named = jnp.sum(named, axis=0, keepdims=True)
            total = jnp.where(belongs & (step == s), named, total)
        return jnp.sum(total, axis=1, keepdims=True)

    for j in range(local):
        if j % 2 == 0 or local % 2:
            share = share_of(lax.div(first + j, 2))
        gate = jnp.dot(lhs[...], wg[j], preferred_element_type=jnp.float32)
        up = jnp.dot(lhs[...], wu[j], preferred_element_type=jnp.float32)
        hidden = gate / (1.0 + jnp.exp(-gate)) * up * share
        hid[:, j * width : (j + 1) * width] = hidden.astype(jnp.bfloat16)
    chunk = 512
    for n in range(wd.shape[1] // chunk):
        span = slice(n * chunk, (n + 1) * chunk)
        out = jnp.dot(hid[...], wd[:, span], preferred_element_type=jnp.float32)
        keep[:, span] = out[:half]
        send[:, span] = out[half:].astype(send.dtype)


def column_sum_kernel(geo, tokens, *refs):
    kept, received = refs[:2]
    outs, wide = refs[2:-1], refs[-1]
    far, near, side, core = geo.here()
    starts = [geo.column_at(near, side, shift, 1) for shift in geo.shifts]
    for k in range(wide.shape[0]):
        lanes = slice(k * 128, (k + 1) * 128)
        wide[k] = kept[:, lanes] + received[:, lanes].astype(jnp.float32)
        for q, start in enumerate(starts):
            picked = wide[k, pl.ds(start, tokens * geo.far, stride=geo.columns), :]
            outs[q][:, lanes] = picked.astype(outs[q].dtype)


def far_sum_kernel(geo, tokens, *refs):
    ins = refs[: geo.columns]
    outs, wide = refs[geo.columns : -1], refs[-1]
    far, near, side, core = geo.here()
    starts = [geo.far_at(far, step, 1) for step in range(geo.far)]
    for k in range(wide.shape[0]):
        lanes = slice(k * 128, (k + 1) * 128)
        total = ins[0][:, lanes]
        for other in ins[1:]:
            total = total + other[:, lanes].astype(jnp.float32)
        wide[k] = total
        for step, start in enumerate(starts):
            picked = wide[k, pl.ds(start, tokens, stride=geo.far), :]
            outs[step][:, lanes] = picked.astype(outs[step].dtype)


def final_kernel(*refs):
    o_ref = refs[-1]
    total = refs[0][...]
    for other in refs[1:-1]:
        total = total + other[...].astype(jnp.float32)
    o_ref[...] = total.astype(o_ref.dtype)


def body(
    geo,
    hidden_in,
    queries,
    new_keys,
    new_values,
    key_cache,
    value_cache,
    cache_lengths,
    page_table,
    o_proj,
    norm_gain,
    expert_ids,
    gate_scores,
    w_gate,
    w_up,
    w_down,
):
    requests, steps = queries.shape[:2]
    tokens = requests * steps
    depth = norm_gain.shape[0]
    col_width = hidden_in.shape[2]
    places = geo.places
    bf16, f32 = jnp.bfloat16, jnp.float32
    core = lax.rem(lax.axis_index("tp"), CORES) if col_width % 128 else None

    def swap(array):
        return lax.ppermute(array, AXES, geo.to_partner())

    o_partner = swap(o_proj)
    if col_width % 128 == 0:
        h_own = hidden_in.reshape(CORES * tokens * places, col_width)
        h_partner = swap(h_own)
    else:
        hidden = hidden_in.reshape(places, CORES, requests, steps, col_width)
        hidden = hidden.transpose(1, 2, 3, 0, 4).reshape(CORES, tokens * places, col_width)
        h_own = jnp.where(core == 0, hidden[0], hidden[1])
        h_partner = swap(jnp.where(core == 0, hidden[1], hidden[0]))

    rows = HQ * tokens
    q = queries.reshape(tokens, HQ, HD).transpose(1, 0, 2).reshape(rows, HD)
    pool = key_cache.shape[0]
    padded = pool + 128 * -(-tokens // 128)
    attended = call(
        functools.partial(attention_kernel, steps),
        "attention",
        jax.ShapeDtypeStruct((rows, HD), bf16),
        [SM] + [HBM] * 6,
        [
            pltpu.VMEM(page_table.shape, jnp.int32),
            pltpu.VMEM((rows, HD), bf16),
            pltpu.VMEM((tokens, key_cache.shape[1]), bf16),
            pltpu.VMEM((tokens, key_cache.shape[1]), bf16),
            pltpu.VMEM((padded, key_cache.shape[1]), bf16),
            pltpu.VMEM((padded, key_cache.shape[1]), bf16),
            pltpu.SemaphoreType.DMA((6,)),
        ],
    )(
        cache_lengths,
        *(
            in_hbm(array)
            for array in (
                page_table,
                q,
                new_keys.reshape(tokens, -1),
                new_values.reshape(tokens, -1),
                key_cache,
                value_cache,
            )
        )
    )

    def gather_far(piece, after, weight):
        got = [piece] + [lax.ppermute(piece, AXES, geo.along_far(s)) for s in range(1, geo.far)]
        return call(
            functools.partial(stack_kernel, geo.far),
            "stack",
            jax.ShapeDtypeStruct((geo.far,) + piece.shape, piece.dtype),
            [VM] * geo.far,
        )(*got)

    def gather_column(stacked):
        return [stacked] + [
            lax.ppermute(stacked, AXES, geo.along_column(shift)) for shift in geo.shifts[1:]
        ]

    stacked = gather_far(attended, None, None)
    pieces = gather_column(stacked)
    residual = call(
        functools.partial(project_kernel, geo, tokens),
        "project",
        jax.ShapeDtypeStruct((tokens * places, CORES * col_width), bf16),
        [VM] * (geo.columns + 4),
        [
            pltpu.VMEM((places * rows, HD), f32),
            pltpu.VMEM((tokens * places, HQ * HD), bf16),
            pltpu.VMEM((CORES * tokens * places, 128), f32),
        ],
    )(*pieces, o_proj, o_partner, h_own, h_partner)
    pieces = gather_column(gather_far(residual, None, None))
    if CORES * col_width % 128:
        pieces = [geo.in_order(jnp.stack(pieces))[None]]
    normed, own_residual = call(
        functools.partial(norm_kernel, geo, tokens),
        "norm",
        [
            jax.ShapeDtypeStruct((tokens * places, depth), bf16),
            jax.ShapeDtypeStruct((tokens, depth), f32),
        ],
        [VM] * (len(pieces) + 1),
        [pltpu.VMEM((tokens * places, depth), f32)],
    )(*pieces, norm_gain.reshape(depth // 128, 128))
    normed_partner = swap(normed)
    local, half = w_gate.shape[0], w_gate.shape[2]
    keep, send = call(
        functools.partial(expert_kernel, geo),
        "experts",
        [
            jax.ShapeDtypeStruct((tokens * places, depth), f32),
            jax.ShapeDtypeStruct((tokens * places, depth), bf16),
        ],
        [VM] * 7,
        [
            pltpu.VMEM((CORES * tokens * places, depth), bf16),
            pltpu.VMEM((CORES * tokens * places, local * half), bf16),
        ],
    )(
        normed,
        normed_partner,
        expert_ids.transpose(0, 2, 1),
        gate_scores.transpose(0, 2, 1),
        in_vmem(w_gate),
        in_vmem(w_up),
        in_vmem(w_down.reshape(local * half, depth)),
    )
    received = swap(send)
    parts = call(
        functools.partial(column_sum_kernel, geo, tokens),
        "column_sum",
        [
            jax.ShapeDtypeStruct((tokens * geo.far, depth), f32 if q == 0 else bf16)
            for q in range(geo.columns)
        ],
        [VM, VM],
        [pltpu.VMEM((depth // 128, tokens * places, 128), f32)],
    )(keep, received)
    parts = [parts[0]] + [
        lax.ppermute(part, AXES, geo.along_column(shift))
        for part, shift in zip(parts[1:], geo.shifts[1:])
    ]
    parts = call(
        functools.partial(far_sum_kernel, geo, tokens),
        "far_sum",
        [
            jax.ShapeDtypeStruct((tokens, depth), f32 if s == 0 else bf16)
            for s in range(geo.far)
        ],
        [VM] * geo.columns,
        [pltpu.VMEM((depth // 128, tokens * geo.far, 128), f32)],
    )(*parts)
    parts = [parts[0]] + [
        lax.ppermute(part, AXES, geo.along_far(step + 1)) for step, part in enumerate(parts[1:])
    ]
    out = call(
        final_kernel,
        "final",
        jax.ShapeDtypeStruct((tokens, depth), bf16),
        [VM] * (geo.far + 1),
    )(own_residual, *parts)
    return out.reshape(requests, steps, depth)


def solution(mesh):
    geo = Geometry(mesh.shape["ep"], mesh.shape["tp"])
    in_specs = (
        P("group", None, ("ep", "tp")),
        P(("group", "ep", "tp"), None, None),
        P(("group", "ep", "tp"), None, None),
        P(("group", "ep", "tp"), None, None),
        P(("group", "ep", "tp"), None),
        P(("group", "ep", "tp"), None),
        P(("group", "ep", "tp")),
        P(("group", "ep", "tp"), None),
        P(None, ("ep", "tp")),
        P(),
        P(None, "group", None),
        P(None, "group", None),
        P(("ep", "tp"), None, None),
        P(("ep", "tp"), None, None),
        P(("ep", "tp"), None, None),
    )
    out_specs = P(("group", "ep", "tp"), None, None)
    return jax.shard_map(
        functools.partial(body, geo),
        mesh=mesh,
        in_specs=in_specs,
        out_specs=out_specs,
        check_vma=False,
    )
```
